32 devices in a mesh: box: 8 (over z, core), dir: 4 (over y, x).
Axes of the slice: x: 2, y: 2, z: 4, core: 2. Of those that a mesh axis runs over, the one named last changes fastest.
Arguments:
- child_out: bfloat16 [1024, 8, 512], P('box', None, 'dir'), may hold values from -6 to 6
- interp: bfloat16 [512, 2048], replicated, may hold values from -0.25 to 0.25
- shift_angle: float32 [8, 2048], replicated, may hold values from -3.140625 to 3.140625
- translators: float32 [343, 2, 2048], P(None, None, 'dir'), may hold values from -3 to 3
- nbr_index: int32 [128, 27], replicated, may hold values from 0 to 127, as said below
- nbr_trans: int32 [128, 27], replicated, may hold values from 0 to 342, as said below
Outputs:
- child_in: bfloat16 [1024, 8, 512], P('box', None, 'dir')
The draws below stay inside these ranges and needn't reach their ends.
Inputs may be any that keep to these rules, and one draw needn't show every extreme that they name: Parents lie on a periodic slab indexed in Morton order: all index bits but the top two are taken in turn by the first two coordinates (lowest bit first), and the top two bits give the third coordinate, which thus runs over 4 layers. Row p holds 27 distinct offsets of largest component 2 or 3, and nbr_index[p, n] is the parent at that offset from p, coordinates taken periodically. nbr_trans[p, n] = (dx + 3) * 49 + (dy + 3) * 7 + (dz + 3) for the offset (dx, dy, dz) of nbr_index[p, n].
All inputs are finite; a program needn't handle non-finite values.
Results may differ from the reference program's by a relative error of at most 0.012.
Values may be sent and summed in bfloat16 or wider, within the bound.
No kernel may reach another device: no remote copies, remote signals or barrier semaphores. Data moves between devices by JAX's collectives and lax.ppermute only.
A program may use at most 64 MiB of HBM per device.

```python
import jax
import jax.numpy as jnp
import numpy as np
from jax import lax

NCD = 512
NPD = 2048
CH = 8
NBR = 27
NT = 343
OCT = 8
COLS = 8
NP = 128
NB = 1024


def partner_lists(key):
    inner = jax.random.fold_in(key, 7)
    bits = max(NP - 1, 1).bit_length()
    assign = [(bit % 2, bit // 2) for bit in range(bits - 2)] + [(2, 0), (2, 1)]
    index = jnp.arange(NP, dtype=jnp.int32)
    coords = [jnp.zeros((NP,), jnp.int32) for axis_num in range(3)]
    counts = [0, 0, 0]
    for bit in range(bits):
        which, level = assign[bit]
        coords[which] = coords[which] + index // 2 ** bit % 2 * 2 ** level
        counts[which] = counts[which] + 1
    extents = [2 ** counts[axis_num] for axis_num in range(3)]
    offsets = []
    for dx in range(-3, 4):
        for dy in range(-3, 4):
            for dz in range(-3, 4):
                if max(abs(dx), abs(dy), abs(dz)) >= 2:
                    offsets.append([dx, dy, dz, (dx + 3) * 49 + (dy + 3) * 7 + (dz + 3)])
    offsets = jnp.asarray(np.array(offsets, dtype=np.int32))
    count = offsets.shape[0]
    scores = jax.random.randint(inner, (NP, count), 0, 2 ** 20) * 512 + jnp.arange(count, dtype=jnp.int32)[None, :]
    chosen = lax.top_k(scores, NBR)[1]
    picked = offsets[chosen]
    moved = [(coords[axis_num][:, None] + picked[:, :, axis_num]) % extents[axis_num] for axis_num in range(3)]
    target = jnp.zeros((NP, NBR), jnp.int32)
    for bit in range(bits):
        which, level = assign[bit]
        target = target + moved[which] // 2 ** level % 2 * 2 ** bit
    return ((target % NP).astype(jnp.int32), picked[:, :, 3].astype(jnp.int32))


def draw_nbr_index(key, part):
    return partner_lists(key)[0]


def draw_nbr_trans(key, part):
    return partner_lists(key)[1]


def block_levels(rng, shape, shards, low, high):
    gain = 1.0
    for position, blocks in shards:
        heights = jax.random.uniform(jax.random.fold_in(jax.random.fold_in(rng, 6), position), (blocks,), jnp.float32, low / len(shards), high / len(shards))
        gain = gain * jnp.repeat(jnp.exp(heights), shape[position] // blocks).reshape((-1,) + (1,) * (len(shape) - 1 - position))
    return gain


def centred(own_key, extent, spread, bound, shards=(), kind=jnp.bfloat16):
    values = spread * jax.random.normal(own_key, extent, jnp.float32)
    if shards:
        values = values * block_levels(own_key, extent, shards, -0.22, 0.18)
    return jnp.clip(values, -bound, bound).astype(kind)


def setup_inputs(seed: int = 0) -> dict:
    arg_keys = jax.random.split(jax.random.key(seed), 7)
    child_out = centred(arg_keys[0], (NB, COLS, NCD), 1.0, 6.0, ((0, 8), (2, 4)))
    interp = centred(arg_keys[1], (NCD, NPD), NCD ** -0.5, 0.25)
    shift_angle = jnp.clip(jax.random.uniform(arg_keys[2], (OCT, NPD), jnp.float32, -3.140625, 3.140625), -3.140625, 3.140625)
    translators = centred(arg_keys[3], (NT, 2, NPD), 0.2, 3.0, ((2, 4),), jnp.float32)
    nbr_index = draw_nbr_index(jax.random.fold_in(arg_keys[6], 71), 0)
    nbr_trans = draw_nbr_trans(jax.random.fold_in(arg_keys[6], 71), 0)
    return dict(child_out=child_out, interp=interp, shift_angle=shift_angle, translators=translators, nbr_index=nbr_index, nbr_trans=nbr_trans)


def cmul(field, real_part, imag_part):
    half = field.shape[-2] // 2
    left = field[..., :half, :]
    right = field[..., half:, :]
    return jnp.concatenate([left * real_part - right * imag_part, left * imag_part + right * real_part], axis=-2)


def reference(child_out, interp, shift_angle, translators, nbr_index, nbr_trans):
    cols = child_out.shape[1]
    interp_child = jnp.dot(child_out.reshape(NB * cols, NCD), interp, preferred_element_type=jnp.float32).reshape(NB, cols, NPD)
    octants = (jnp.arange(NB, dtype=jnp.int32) % CH).astype(jnp.int32)
    cosine = jnp.cos(shift_angle)[octants][:, None, :]
    sine = jnp.sin(shift_angle)[octants][:, None, :]
    shifted = cmul(interp_child, cosine, sine)
    parent_out = shifted.reshape(NP, CH, cols, NPD).sum(axis=1).astype(jnp.bfloat16)
    parent_in = jnp.zeros((NP, cols, NPD), jnp.float32)
    for slot in range(NBR):
        source = parent_out[nbr_index[:, slot]].astype(jnp.float32)
        table = translators[nbr_trans[:, slot]]
        parent_in = parent_in + cmul(source, table[:, 0:1, :], table[:, 1:2, :])
    parent_in = parent_in.astype(jnp.bfloat16)
    down = jnp.repeat(parent_in, CH, axis=0).astype(jnp.float32)
    back = cmul(down, cosine, -sine).astype(jnp.bfloat16)
    result = jnp.dot(back.reshape(NB * cols, NPD), interp.T, preferred_element_type=jnp.float32)
    return (0.125 * result).reshape(NB, cols, NCD).astype(jnp.bfloat16)
```

```python
import functools

import jax
import jax.numpy as jnp
from jax import lax
from jax.experimental import pallas as pl
from jax.experimental.pallas import tpu as pltpu
from jax.sharding import PartitionSpec as P

CH = 8
LANES = 128
anterp_scale = 0.125

VMEM = pl.BlockSpec(memory_space=pltpu.VMEM)
SMEM = pl.BlockSpec(memory_space=pltpu.SMEM)


def half_sign(rows, first):
    row = lax.broadcasted_iota(jnp.int32, (rows, LANES), 0)
    return jnp.where(row < rows // 2, first, -first).astype(jnp.float32)


def forward_kernel(masks, chunks, at_ref, x_ref, interp_ref, cos_ref, sin_ref, *rest):
    outs, field = rest[: len(masks)], rest[len(masks)]
    par_cnt, cols = outs[0].shape[1], outs[0].shape[2]
    width = chunks * LANES
    sign = half_sign(cols, -1.0)
    for mask, out_ref in zip(masks, outs):
        start = pl.multiple_of((at_ref[0] ^ mask) * width, width)
        field[...] = jnp.dot(
            x_ref[...], interp_ref[:, pl.ds(start, width)], preferred_element_type=jnp.float32
        )
        for chunk in range(chunks):
            lanes = pl.ds(pl.multiple_of(start + chunk * LANES, LANES), LANES)
            cosine = jnp.broadcast_to(cos_ref[:, lanes][:, None, :], (CH, cols, LANES))
            sine = jnp.broadcast_to(sin_ref[:, lanes][:, None, :], (CH, cols, LANES))

            def one(p, carry, chunk=chunk, cosine=cosine, sine=sine, out_ref=out_ref):
                rows = pl.ds(pl.multiple_of(p * CH * cols, CH * cols), CH * cols)
                part = field[rows, chunk * LANES : (chunk + 1) * LANES].reshape(CH, cols, LANES)
                same = jnp.sum(part * cosine, axis=0)
                cross = jnp.sum(part * sine, axis=0)
                total = same + sign * pltpu.roll(cross, cols // 2, 0)
                out_ref[chunk, p] = total.astype(out_ref.dtype)
                return carry

            lax.fori_loop(0, par_cnt, one, 0, unroll=4)


def forward(masks, chunks, at, x, interp, cosine, sine, cols):
    rows = x.shape[0]
    par_cnt = rows // (CH * cols)
    shape = (chunks, par_cnt, cols, LANES)
    return pl.pallas_call(
        functools.partial(forward_kernel, masks, chunks),
        out_shape=[
            jax.ShapeDtypeStruct(shape, jnp.bfloat16 if mask else jnp.float32) for mask in masks
        ],
        in_specs=[SMEM, VMEM, VMEM, VMEM, VMEM],
        out_specs=[VMEM] * len(masks),
        scratch_shapes=[pltpu.VMEM((rows, chunks * LANES), jnp.float32)],
        name="forward",
    )(at, x, interp, cosine, sine)


def translate_kernel(zc, rest, slots, at_ref, picks_ref, table_ref, *refs):
    count = len(refs) - zc - 1
    pieces, outs, source = refs[:count], refs[count : count + zc], refs[count + zc]
    par_cnt, cols = outs[0].shape[0], outs[0].shape[1]
    zi, ci = at_ref[0], at_ref[1]
    each = count // zc
    for s in range(zc):
        for t in range(each):
            box = (zi ^ s) * rest + ((ci ^ t) if each > 1 else 0)
            piece = pieces[s * each + t]
            here = piece.shape[0]
            source[pl.ds(box * par_cnt, here)] = piece[...].astype(jnp.float32)
    sign = half_sign(cols, -1.0)
    for s in range(zc):
        first = ((zi ^ s) * rest + ci) * par_cnt

        def one(p, carry, first=first, out_ref=outs[s]):
            same = jnp.zeros((cols, LANES), jnp.float32)
            cross = jnp.zeros((cols, LANES), jnp.float32)
            for slot in range(slots):
                word = picks_ref[slot, first + p]
                which, offset = word & 0xFFFF, word >> 16
                value = source[which]
                real = table_ref[pl.ds(offset, 1), :]
                imag = table_ref[pl.ds(offset + 1, 1), :]
                same += value * real
                cross += value * imag
            total = same + sign * pltpu.roll(cross, cols // 2, 0)
            out_ref[p] = total.astype(out_ref.dtype)
            return carry

        lax.fori_loop(0, par_cnt, one, 0)


def translate(zc, rest, par_cnt, at, picks, table, pieces):
    cols, lanes = pieces[0].shape[1:]
    return pl.pallas_call(
        functools.partial(translate_kernel, zc, rest, picks.shape[0]),
        out_shape=[jax.ShapeDtypeStruct((par_cnt, cols, lanes), jnp.bfloat16)] * zc,
        in_specs=[SMEM, SMEM, VMEM] + [VMEM] * len(pieces),
        out_specs=[VMEM] * zc,
        scratch_shapes=[pltpu.VMEM((zc * rest * par_cnt, cols, lanes), jnp.float32)],
        name="translate",
    )(at, picks, table, *pieces)


def backward_kernel(masks, wide, last, at_ref, interp_ref, cos_ref, sin_ref, *refs):
    quarters = refs[: len(masks)]
    held = refs[len(masks)] if len(refs) == len(masks) + 4 else None
    out_ref, left, right = refs[-3:]
    chunks, par_cnt, cols, _ = quarters[0].shape
    width = chunks * LANES
    sign = half_sign(cols, 1.0)
    total = None
    for mask, quarter in zip(masks, quarters):
        for chunk in range(chunks):
            place = (at_ref[1] ^ (chunk // wide)) * wide + chunk % wide
            start = (at_ref[0] ^ mask) * width + place * LANES
            lanes = pl.ds(pl.multiple_of(start, LANES), LANES)
            cosine = jnp.broadcast_to(cos_ref[:, lanes][:, None, :], (CH, cols, LANES))
            sine = jnp.broadcast_to(sin_ref[:, lanes][:, None, :], (CH, cols, LANES)) * sign[None]
            here = slice(chunk * LANES, (chunk + 1) * LANES)
            right[:, here] = interp_ref[:, lanes]

            def one(p, carry, chunk=chunk, cosine=cosine, sine=sine, here=here, quarter=quarter):
                field = quarter[chunk, p].astype(jnp.float32)
                turned = pltpu.roll(field, cols // 2, 0)
                moved = field[None] * cosine + turned[None] * sine
                rows = pl.ds(pl.multiple_of(p * CH * cols, CH * cols), CH * cols)
                left[rows, here] = moved.reshape(CH * cols, LANES).astype(jnp.bfloat16)
                return carry

            lax.fori_loop(0, par_cnt, one, 0, unroll=4)
        part = lax.dot_general(
            left[...], right[...], (((1,), (1,)), ((), ())), preferred_element_type=jnp.float32
        )
        total = part if total is None else total + part
    if held is not None:
        total = total + held[...]
    if last:
        total = anterp_scale * total
    out_ref[...] = total.astype(out_ref.dtype)


def backward(masks, wide, last, at, interp, cosine, sine, quarters, held):
    chunks, par_cnt, cols, _ = quarters[0].shape
    rows = par_cnt * CH * cols
    kept = [] if held is None else [held]
    return pl.pallas_call(
        functools.partial(backward_kernel, masks, wide, last),
        out_shape=jax.ShapeDtypeStruct(
            (rows, interp.shape[0]), jnp.bfloat16 if last else jnp.float32
        ),
        in_specs=[SMEM, VMEM, VMEM, VMEM] + [VMEM] * (len(masks) + len(kept)),
        out_specs=VMEM,
        scratch_shapes=[
            pltpu.VMEM((rows, chunks * LANES), jnp.bfloat16),
            pltpu.VMEM((interp.shape[0], chunks * LANES), jnp.bfloat16),
        ],
        name="backward",
    )(at, interp, cosine, sine, *quarters, *kept)


def exchange(value, axis, mask):
    size = lax.axis_size(axis)
    return lax.ppermute(value, axis, [(i, i ^ mask) for i in range(size)])


def per_device(child_out, interp, shift_angle, translators, nbr_index, nbr_trans):
    child_cnt, cols, kq = child_out.shape
    par_cnt = child_cnt // CH
    npd = interp.shape[1]
    ndir, nbox = lax.axis_size("dir"), lax.axis_size("box")
    jq = npd // ndir
    zc = 1
    while nbox % (2 * zc) == 0 and zc * 2 < nbox and jq % (2 * zc * LANES) == 0:
        zc *= 2
    rest = nbox // zc
    chunks = jq // LANES
    dir_at, box_at = lax.axis_index("dir"), lax.axis_index("box")
    zi, ci = box_at // rest, box_at % rest
    at = jnp.stack([dir_at, zi, ci]).astype(jnp.int32)

    x = child_out.reshape(child_cnt * cols, kq)
    mine = lax.dynamic_slice_in_dim(interp, dir_at * kq, kq, 0)
    cosine, sine = jnp.cos(shift_angle), jnp.sin(shift_angle)

    masks = tuple(range(1, ndir)) + (0,)
    parts = forward(masks, chunks, at, x, mine, cosine, sine, cols)
    total = parts[-1]
    for mask, part in zip(masks[:-1], parts):
        total = total + exchange(part, "dir", mask).astype(jnp.float32)
    own = total.astype(jnp.bfloat16).reshape(zc, chunks // zc, par_cnt, cols, LANES)

    wide = chunks // zc
    pieces = []
    for s in range(zc):
        piece = lax.dynamic_index_in_dim(own, zi ^ s, 0, keepdims=False)
        pieces.append(exchange(piece, "box", s * rest) if s else piece)

    table = lax.dynamic_slice_in_dim(translators, zi * wide * LANES, wide * LANES, 2)
    picks = (nbr_index | (nbr_trans * 2 << 16)).T

    if rest == 2:
        pieces = [part for piece in pieces for part in (piece, exchange(piece, "box", 1))]
    else:
        groups = [[z * rest + c for c in range(rest)] for z in range(zc)]
        pieces = [
            lax.all_gather(piece, "box", axis=1, tiled=True, axis_index_groups=groups)
            for piece in pieces
        ]
    back = []
    for w in range(wide):
        rows = table[:, :, w * LANES : (w + 1) * LANES].reshape(-1, LANES)
        parts = [piece[w] for piece in pieces]
        back.append(translate(zc, rest, par_cnt, at[1:], picks, rows, parts))
    quarter = []
    for s in range(zc):
        result = jnp.stack([b[s] for b in back])
        quarter.append(exchange(result, "box", s * rest) if s else result)
    quarter = jnp.concatenate(quarter, 0)

    quarters = [exchange(quarter, "dir", mask) for mask in range(1, ndir)]
    held = backward((0,), wide, False, at, mine, cosine, sine, [quarter], None)
    out = backward(tuple(range(1, ndir)), wide, True, at, mine, cosine, sine, quarters, held)
    return out.reshape(child_cnt, cols, kq)


def solution(mesh):
    in_specs = (P("box", None, "dir"), P(), P(), P(None, None, "dir"), P(), P())
    out_specs = P("box", None, "dir")
    return jax.shard_map(
        per_device, mesh=mesh, in_specs=in_specs, out_specs=out_specs, check_vma=False
    )
```

```python
import functools

import jax
import jax.numpy as jnp
from jax import lax
from jax.experimental import pallas as pl
from jax.experimental.pallas import tpu as pltpu
from jax.sharding import PartitionSpec as P


CH = 8
LANES = 128
anterp_scale = 0.125
HALF_PI = 1.5707963267948966
HALF_PI_HIGH = 1.57080078125
HALF_PI_LOW = HALF_PI - HALF_PI_HIGH

VMEM = pl.BlockSpec(memory_space=pltpu.VMEM)
SMEM = pl.BlockSpec(memory_space=pltpu.SMEM)
FAR = pl.BlockSpec(memory_space=pltpu.HBM)
GRANT = pltpu.CompilerParams(vmem_limit_bytes=12 << 20)


def half_sign(rows, first):
    row = lax.broadcasted_iota(jnp.int32, (rows, LANES), 0)
    return jnp.where(row < rows // 2, first, -first).astype(jnp.float32)


def sine_cosine(angle):
    turns = jnp.round(angle * (1.0 / HALF_PI))
    x = (angle - turns * HALF_PI_HIGH) - turns * HALF_PI_LOW
    y = x * x
    s = x * (1.0 + y * (-1.6666654611e-1 + y * (8.3321608736e-3 + y * -1.9515295891e-4)))
    c = 1.0 + y * (
        -0.5 + y * (4.166664568298827e-2 + y * (-1.388731625493765e-3 + y * 2.443315711809948e-5))
    )
    quadrant = turns.astype(jnp.int32)
    odd = (quadrant & 1) == 1
    sine = jnp.where(odd, c, s)
    cosine = jnp.where(odd, s, c)
    sine = jnp.where((quadrant & 2) == 2, -sine, sine)
    cosine = jnp.where(((quadrant + 1) & 2) == 2, -cosine, cosine)
    return sine, cosine


def add_octants(start, x_ref, interp_ref, cos_ref, sin_ref, out_ref, field):
    chunks, par_cnt, cols, _ = out_ref.shape
    width = chunks * LANES
    sign = half_sign(cols, -1.0)
    field[...] = jnp.dot(
        x_ref[...], interp_ref[:, pl.ds(start, width)], preferred_element_type=jnp.float32
    )
    for chunk in range(chunks):
        lanes = pl.ds(pl.multiple_of(start + chunk * LANES, LANES), LANES)
        cosine = jnp.broadcast_to(cos_ref[:, lanes][:, None, :], (CH, cols, LANES))
        sine = jnp.broadcast_to(sin_ref[:, lanes][:, None, :], (CH, cols, LANES))

        def one(p, carry, chunk=chunk, cosine=cosine, sine=sine):
            rows = pl.ds(pl.multiple_of(p * CH * cols, CH * cols), CH * cols)
            part = field[rows, chunk * LANES : (chunk + 1) * LANES].reshape(CH, cols, LANES)
            same = jnp.sum(part * cosine, axis=0)
            cross = jnp.sum(part * sine, axis=0)
            total = same + sign * pltpu.roll(cross, cols // 2, 0)
            out_ref[chunk, p] = total.astype(out_ref.dtype)
            return carry

        lax.fori_loop(0, par_cnt, one, 0, unroll=4)


def first_kernel(mask, at_ref, x_any, interp_any, angle_any, *refs):
    out_ref, x_ref, interp_ref, cos_ref, sin_ref, field, angle_ref, sems = refs
    load_angle = pltpu.make_async_copy(angle_any, angle_ref, sems.at[2])
    load_angle.start()
    width = out_ref.shape[0] * LANES
    rows = interp_ref.shape[0]
    dir_at = at_ref[0]
    start = pl.multiple_of((dir_at ^ mask) * width, width)
    mine = pl.ds(pl.multiple_of(dir_at * rows, rows), rows)
    load_x = pltpu.make_async_copy(x_any, x_ref, sems.at[0])
    load_interp = pltpu.make_async_copy(interp_any.at[mine], interp_ref, sems.at[1])
    load_x.start()
    load_interp.start()
    load_angle.wait()
    sine, cosine = sine_cosine(angle_ref[...])
    cos_ref[...] = cosine
    sin_ref[...] = sine
    load_x.wait()
    load_interp.wait()
    add_octants(start, x_ref, interp_ref, cos_ref, sin_ref, out_ref, field)


def first_forward(mask, chunks, cols, at, x, interp, angle):
    rows, kq = x.shape
    npd = interp.shape[1]
    par_cnt = rows // (CH * cols)
    return pl.pallas_call(
        functools.partial(first_kernel, mask),
        out_shape=[
            jax.ShapeDtypeStruct((chunks, par_cnt, cols, LANES), jnp.bfloat16),
            jax.ShapeDtypeStruct(x.shape, x.dtype),
            jax.ShapeDtypeStruct((kq, npd), interp.dtype),
            jax.ShapeDtypeStruct(angle.shape, jnp.float32),
            jax.ShapeDtypeStruct(angle.shape, jnp.float32),
        ],
        in_specs=[SMEM, FAR, FAR, FAR],
        out_specs=[VMEM] * 5,
        scratch_shapes=[
            pltpu.VMEM((rows, chunks * LANES), jnp.float32),
            pltpu.VMEM(angle.shape, jnp.float32),
            pltpu.SemaphoreType.DMA((3,)),
        ],
        compiler_params=GRANT,
        name="first_forward",
    )(at, x, interp, angle)


def forward_kernel(mask, at_ref, x_ref, interp_ref, cos_ref, sin_ref, out_ref, field):
    width = out_ref.shape[0] * LANES
    start = pl.multiple_of((at_ref[0] ^ mask) * width, width)
    add_octants(start, x_ref, interp_ref, cos_ref, sin_ref, out_ref, field)


def forward(mask, chunks, cols, at, x, interp, cosine, sine):
    rows = x.shape[0]
    shape = (chunks, rows // (CH * cols), cols, LANES)
    return pl.pallas_call(
        functools.partial(forward_kernel, mask),
        out_shape=jax.ShapeDtypeStruct(shape, jnp.bfloat16 if mask else jnp.float32),
        in_specs=[SMEM, VMEM, VMEM, VMEM, VMEM],
        out_specs=VMEM,
        scratch_shapes=[pltpu.VMEM((rows, chunks * LANES), jnp.float32)],
        compiler_params=GRANT,
        name="forward",
    )(at, x, interp, cosine, sine)


def last_forward_kernel(wide, at_ref, x_ref, interp_ref, cos_ref, sin_ref, *refs):
    tables_any, which_any, offset_any, out_ref, rows_ref, which_ref, offset_ref, field, sems = refs
    width = out_ref.shape[0] * LANES
    lanes = pl.ds(pl.multiple_of(at_ref[1] * wide * LANES, LANES), wide * LANES)
    loads = [
        pltpu.make_async_copy(tables_any.at[:, :, lanes], rows_ref, sems.at[0]),
        pltpu.make_async_copy(which_any, which_ref, sems.at[1]),
        pltpu.make_async_copy(offset_any, offset_ref, sems.at[2]),
    ]
    for load in loads:
        load.start()
    start = pl.multiple_of(at_ref[0] * width, width)
    add_octants(start, x_ref, interp_ref, cos_ref, sin_ref, out_ref, field)
    for load in loads:
        load.wait()


def last_forward(chunks, wide, cols, at, x, interp, cosine, sine, tables, which, offset):
    rows = x.shape[0]
    return pl.pallas_call(
        functools.partial(last_forward_kernel, wide),
        out_shape=[
            jax.ShapeDtypeStruct((chunks, rows // (CH * cols), cols, LANES), jnp.float32),
            jax.ShapeDtypeStruct(tables.shape[:2] + (wide * LANES,), tables.dtype),
            pltpu.SMEM(which.shape, which.dtype),
            pltpu.SMEM(offset.shape, offset.dtype),
        ],
        in_specs=[SMEM, VMEM, VMEM, VMEM, VMEM, FAR, FAR, FAR],
        out_specs=[VMEM, VMEM, SMEM, SMEM],
        scratch_shapes=[
            pltpu.VMEM((rows, chunks * LANES), jnp.float32),
            pltpu.SemaphoreType.DMA((3,)),
        ],
        compiler_params=GRANT,
        name="last_forward",
    )(at, x, interp, cosine, sine, tables, which, offset)


def gather_kernel(zc, rest, at_ref, *refs):
    pieces, source = refs[:-1], refs[-1]
    each = len(pieces) // zc
    cols = pieces[0].shape[1]
    own = pieces[0].shape[0] if each > 1 else pieces[0].shape[0] // rest
    zi, ci = at_ref[1], at_ref[2]
    for s in range(zc):
        for t in range(each):
            box = (zi ^ s) * rest + ((ci ^ t) if each > 1 else 0)
            piece = pieces[s * each + t]
            here = piece.shape[0] * cols
            rows = pl.ds(pl.multiple_of(box * own * cols, cols), here)
            source[rows, :] = piece[...].astype(jnp.float32).reshape(here, LANES)


def add_partners(targets, rest, at_ref, which_ref, offset_ref, table_ref, source, outs):
    par_cnt, cols = outs[0].shape[:2]
    total_cnt = source.shape[0] // cols
    slots = which_ref.shape[0] // total_cnt
    zi, ci = at_ref[1], at_ref[2]
    sign = half_sign(cols, -1.0)
    for s, out_ref in zip(targets, outs):
        first = ((zi ^ s) * rest + ci) * par_cnt

        def one(p, carry, first=first, out_ref=out_ref):
            same = jnp.zeros((cols, LANES), jnp.float32)
            cross = jnp.zeros((cols, LANES), jnp.float32)
            for slot in range(slots):
                place = slot * total_cnt + (first + p)
                which = pl.multiple_of(which_ref[place], cols)
                offset = offset_ref[place]
                value = source[pl.ds(which, cols), :]
                same += value * table_ref[offset, 0:1, :]
                cross += value * table_ref[offset, 1:2, :]
            total = same + sign * pltpu.roll(cross, cols // 2, 0)
            out_ref[p] = total.astype(out_ref.dtype)
            return carry

        lax.fori_loop(0, par_cnt, one, 0, unroll=2)


def first_translate_kernel(zc, rest, targets, at_ref, which_ref, offset_ref, table_ref, *refs):
    outs, source = refs[-1 - len(targets) : -1], refs[-1]
    gather_kernel(zc, rest, at_ref, *refs[: -1 - len(targets)], source)
    add_partners(targets, rest, at_ref, which_ref, offset_ref, table_ref, source, outs)


def translate_kernel(rest, targets, at_ref, which_ref, offset_ref, table_ref, source, *outs):
    add_partners(targets, rest, at_ref, which_ref, offset_ref, table_ref, source, outs)


def translate(zc, rest, par_cnt, groups, at, picks, table, pieces):
    cols, lanes = pieces[0].shape[1:]
    out = jax.ShapeDtypeStruct((par_cnt, cols, lanes), jnp.bfloat16)
    found = {}
    source = None
    for targets in groups:
        if source is None:
            result = pl.pallas_call(
                functools.partial(first_translate_kernel, zc, rest, targets),
                out_shape=[out] * len(targets)
                + [jax.ShapeDtypeStruct((zc * rest * par_cnt * cols, lanes), jnp.float32)],
                in_specs=[SMEM, SMEM, SMEM, VMEM] + [VMEM] * len(pieces),
                out_specs=[VMEM] * (len(targets) + 1),
                compiler_params=GRANT,
                name="first_translate",
            )(at, *picks, table, *pieces)
            source = result[-1]
        else:
            call = pl.pallas_call(
                functools.partial(translate_kernel, rest, targets),
                out_shape=[out] * len(targets),
                in_specs=[SMEM, SMEM, SMEM, VMEM, VMEM],
                out_specs=[VMEM] * len(targets),
                compiler_params=GRANT,
                name="translate",
            )
            result = call(at, *picks, table, source)
        for s, value in zip(targets, result):
            found[s] = value
    return [found[s] for s in range(zc)]


def backward_kernel(mask, wide, last, at_ref, interp_ref, cos_ref, sin_ref, quarter, *refs):
    held = refs[0] if len(refs) == 4 else None
    out_ref, left, right = refs[-3:]
    chunks, par_cnt, cols, _ = quarter.shape
    width = chunks * LANES
    sign = half_sign(cols, 1.0)
    for chunk in range(chunks):
        place = (at_ref[1] ^ (chunk // wide)) * wide + chunk % wide
        start = (at_ref[0] ^ mask) * width + place * LANES
        lanes = pl.ds(pl.multiple_of(start, LANES), LANES)
        cosine = jnp.broadcast_to(cos_ref[:, lanes][:, None, :], (CH, cols, LANES))
        sine = jnp.broadcast_to(sin_ref[:, lanes][:, None, :], (CH, cols, LANES)) * sign[None]
        here = slice(chunk * LANES, (chunk + 1) * LANES)
        right[:, here] = interp_ref[:, lanes]

        def one(p, carry, chunk=chunk, cosine=cosine, sine=sine, here=here):
            field = quarter[chunk, p].astype(jnp.float32)
            turned = pltpu.roll(field, cols // 2, 0)
            moved = field[None] * cosine + turned[None] * sine
            rows = pl.ds(pl.multiple_of(p * CH * cols, CH * cols), CH * cols)
            left[rows, here] = moved.reshape(CH * cols, LANES).astype(jnp.bfloat16)
            return carry

        lax.fori_loop(0, par_cnt, one, 0, unroll=4)
    total = lax.dot_general(
        left[...], right[...], (((1,), (1,)), ((), ())), preferred_element_type=jnp.float32
    )
    if held is not None:
        total = total + held[...]
    if last:
        total = anterp_scale * total
    out_ref[...] = total.astype(out_ref.dtype)


def backward(mask, wide, last, at, interp, cosine, sine, quarter, held):
    chunks, par_cnt, cols, _ = quarter.shape
    rows = par_cnt * CH * cols
    kept = [] if held is None else [held]
    return pl.pallas_call(
        functools.partial(backward_kernel, mask, wide, last),
        out_shape=jax.ShapeDtypeStruct(
            (rows, interp.shape[0]), jnp.bfloat16 if last else jnp.float32
        ),
        in_specs=[SMEM, VMEM, VMEM, VMEM, VMEM] + [VMEM] * len(kept),
        out_specs=VMEM,
        scratch_shapes=[
            pltpu.VMEM((rows, chunks * LANES), jnp.bfloat16),
            pltpu.VMEM((interp.shape[0], chunks * LANES), jnp.bfloat16),
        ],
        compiler_params=GRANT,
        name="backward",
    )(at, interp, cosine, sine, quarter, *kept)


def far(value):
    return pltpu.with_memory_space_constraint(value, pltpu.HBM)


def exchange(value, axis, mask):
    size = lax.axis_size(axis)
    return lax.ppermute(value, axis, [(i, i ^ mask) for i in range(size)])


def per_device(child_out, interp, shift_angle, translators, nbr_index, nbr_trans):
    child_cnt, cols, kq = child_out.shape
    par_cnt = child_cnt // CH
    npd = interp.shape[1]
    ndir, nbox = lax.axis_size("dir"), lax.axis_size("box")
    jq = npd // ndir
    zc = 1
    while nbox % (2 * zc) == 0 and zc * 2 < nbox and jq % (2 * zc * LANES) == 0:
        zc *= 2
    rest = nbox // zc
    chunks = jq // LANES
    wide = chunks // zc
    dir_at, box_at = lax.axis_index("dir"), lax.axis_index("box")
    zi, ci = box_at // rest, box_at % rest
    at = jnp.stack([dir_at, zi, ci]).astype(jnp.int32)
    x = child_out.reshape(child_cnt * cols, kq)
    masks = tuple(range(ndir - 1, 0, -1))

    picks = [(nbr_index * cols).T.reshape(-1), nbr_trans.T.reshape(-1)]

    part, x, mine, cosine, sine = first_forward(
        masks[0], chunks, cols, at, far(x), far(interp), far(shift_angle)
    )
    arrived = [exchange(part, "dir", masks[0])]
    for mask in masks[1:]:
        part = forward(mask, chunks, cols, at, x, mine, cosine, sine)
        arrived.append(exchange(part, "dir", mask))
    total, table, *picks = last_forward(
        chunks, wide, cols, at, x, mine, cosine, sine, far(translators), *map(far, picks)
    )
    for part in arrived:
        total = total + part.astype(jnp.float32)
    own = total.astype(jnp.bfloat16).reshape(zc, wide, par_cnt, cols, LANES)

    pieces = []
    for s in range(zc):
        piece = lax.dynamic_index_in_dim(own, zi ^ s, 0, keepdims=False)
        pieces.append(exchange(piece, "box", s * rest) if s else piece)
    if rest == 2:
        pieces = [part for piece in pieces for part in (piece, exchange(piece, "box", 1))]
    else:
        groups = [[z * rest + c for c in range(rest)] for z in range(zc)]
        pieces = [
            lax.all_gather(piece, "box", axis=1, tiled=True, axis_index_groups=groups)
            for piece in pieces
        ]

    order = [(s,) for s in range(zc - 1, -1, -1)]
    back = []
    for w in range(wide):
        rows = table[:, :, w * LANES : (w + 1) * LANES]
        parts = [piece[w] for piece in pieces]
        back.append(translate(zc, rest, par_cnt, order, at, picks, rows, parts))
    quarter = []
    for s in range(zc):
        result = jnp.stack([b[s] for b in back])
        quarter.append(exchange(result, "box", s * rest) if s else result)
    quarter = jnp.concatenate(quarter, 0)

    received = [exchange(quarter, "dir", mask) for mask in range(1, ndir)]
    out = backward(0, wide, ndir == 1, at, mine, cosine, sine, quarter, None)
    for mask, quarter in zip(range(1, ndir), received):
        out = backward(mask, wide, mask == ndir - 1, at, mine, cosine, sine, quarter, out)
    return out.reshape(child_cnt, cols, kq)


def solution(mesh):
    in_specs = (P("box", None, "dir"), P(), P(), P(None, None, "dir"), P(), P())
    out_specs = P("box", None, "dir")

    return jax.shard_map(
        per_device, mesh=mesh, in_specs=in_specs, out_specs=out_specs, check_vma=False
    )
```

```python
import functools

import jax
import jax.numpy as jnp
from jax import lax
from jax.experimental import pallas as pl
from jax.experimental.pallas import tpu as pltpu
from jax.sharding import PartitionSpec as P


CH = 8
LANES = 128
anterp_scale = 0.125
HALF_PI = 1.5707963267948966
HALF_PI_HIGH = 1.57080078125
HALF_PI_LOW = HALF_PI - HALF_PI_HIGH

VMEM = pl.BlockSpec(memory_space=pltpu.VMEM)
SMEM = pl.BlockSpec(memory_space=pltpu.SMEM)
FAR = pl.BlockSpec(memory_space=pltpu.HBM)
GRANT = pltpu.CompilerParams(vmem_limit_bytes=12 << 20)


def places(rest):
    box_at = lax.axis_index("box")
    return lax.axis_index("dir"), box_at // rest, box_at % rest


def half_sign(rows, first):
    row = lax.broadcasted_iota(jnp.int32, (rows, LANES), 0)
    return jnp.where(row < rows // 2, first, -first).astype(jnp.float32)


def sine_cosine(angle):
    turns = jnp.round(angle * (1.0 / HALF_PI))
    x = (angle - turns * HALF_PI_HIGH) - turns * HALF_PI_LOW
    y = x * x
    s = x * (1.0 + y * (-1.6666654611e-1 + y * (8.3321608736e-3 + y * -1.9515295891e-4)))
    c = 1.0 + y * (
        -0.5 + y * (4.166664568298827e-2 + y * (-1.388731625493765e-3 + y * 2.443315711809948e-5))
    )
    quadrant = turns.astype(jnp.int32)
    odd = (quadrant & 1) == 1
    sine = jnp.where(odd, c, s)
    cosine = jnp.where(odd, s, c)
    sine = jnp.where((quadrant & 2) == 2, -sine, sine)
    cosine = jnp.where(((quadrant + 1) & 2) == 2, -cosine, cosine)
    return sine, cosine


def add_octants(start, x_ref, interp_ref, cos_ref, sin_ref, out_ref):
    chunks, par_cnt, cols, _ = out_ref.shape
    span = min(chunks, 2)
    sign = half_sign(cols, -1.0)
    for base in range(0, chunks, span):
        at = pl.multiple_of(start + base * LANES, LANES)
        field = jnp.dot(
            x_ref[...], interp_ref[:, pl.ds(at, span * LANES)], preferred_element_type=jnp.float32
        )
        for chunk in range(span):
            lanes = pl.ds(pl.multiple_of(at + chunk * LANES, LANES), LANES)
            cosine = [jnp.broadcast_to(cos_ref[o : o + 1, lanes], (cols, LANES)) for o in range(CH)]
            sine = [jnp.broadcast_to(sin_ref[o : o + 1, lanes], (cols, LANES)) for o in range(CH)]
            for p in range(par_cnt):
                same = cross = None
                for o in range(CH):
                    row = (p * CH + o) * cols
                    part = field[row : row + cols, chunk * LANES : (chunk + 1) * LANES]
                    same = part * cosine[o] if o == 0 else same + part * cosine[o]
                    cross = part * sine[o] if o == 0 else cross + part * sine[o]
                total = same + sign * pltpu.roll(cross, cols // 2, 0)
                out_ref[base + chunk, p] = total.astype(out_ref.dtype)


def first_kernel(mask, x_any, interp_any, angle_any, *refs):
    out_ref, x_ref, interp_ref, cos_ref, sin_ref, angle_ref, sems = refs
    load_angle = pltpu.make_async_copy(angle_any, angle_ref, sems.at[2])
    load_angle.start()
    width = out_ref.shape[0] * LANES
    rows = interp_ref.shape[0]
    dir_at = lax.axis_index("dir")
    start = pl.multiple_of((dir_at ^ mask) * width, width)
    mine = pl.ds(pl.multiple_of(dir_at * rows, rows), rows)
    load_x = pltpu.make_async_copy(x_any, x_ref, sems.at[0])
    load_interp = pltpu.make_async_copy(interp_any.at[mine], interp_ref, sems.at[1])
    load_x.start()
    load_interp.start()
    load_angle.wait()
    sine, cosine = sine_cosine(angle_ref[...])
    cos_ref[...] = cosine
    sin_ref[...] = sine
    load_x.wait()
    load_interp.wait()
    add_octants(start, x_ref, interp_ref, cos_ref, sin_ref, out_ref)


def first_forward(mask, chunks, cols, x, interp, angle):
    rows, kq = x.shape
    npd = interp.shape[1]
    par_cnt = rows // (CH * cols)
    return pl.pallas_call(
        functools.partial(first_kernel, mask),
        out_shape=[
            jax.ShapeDtypeStruct((chunks, par_cnt, cols, LANES), jnp.bfloat16),
            jax.ShapeDtypeStruct(x.shape, x.dtype),
            jax.ShapeDtypeStruct((kq, npd), interp.dtype),
            jax.ShapeDtypeStruct(angle.shape, jnp.float32),
            jax.ShapeDtypeStruct(angle.shape, jnp.float32),
        ],
        in_specs=[FAR, FAR, FAR],
        out_specs=[VMEM] * 5,
        scratch_shapes=[
            pltpu.VMEM(angle.shape, jnp.float32),
            pltpu.SemaphoreType.DMA((3,)),
        ],
        compiler_params=GRANT,
        name="first_forward",
    )(x, interp, angle)


def forward_kernel(mask, x_ref, interp_ref, cos_ref, sin_ref, out_ref):
    width = out_ref.shape[0] * LANES
    start = pl.multiple_of((lax.axis_index("dir") ^ mask) * width, width)
    add_octants(start, x_ref, interp_ref, cos_ref, sin_ref, out_ref)


def forward(mask, chunks, cols, x, interp, cosine, sine):
    rows = x.shape[0]
    shape = (chunks, rows // (CH * cols), cols, LANES)
    return pl.pallas_call(
        functools.partial(forward_kernel, mask),
        out_shape=jax.ShapeDtypeStruct(shape, jnp.bfloat16 if mask else jnp.float32),
        in_specs=[VMEM, VMEM, VMEM, VMEM],
        out_specs=VMEM,
        compiler_params=GRANT,
        name="forward",
    )(x, interp, cosine, sine)


def one_hot(column, count):
    lane = lax.broadcasted_iota(jnp.int32, (column.shape[0], count), 1)
    return jnp.where(lane == column, 1.0, 0.0).astype(jnp.bfloat16)


def prepare_kernel(zc, rest, wide, words_ref, tables_any, *refs):
    pick_ref, factor_ref, table, sems = refs
    total_cnt, slots = words_ref.shape
    par_cnt = total_cnt // (zc * rest)
    offsets, depth = tables_any.shape[0], table.shape[1]
    _, zi, ci = places(rest)
    loads = []
    table[:, offsets // 8 * 8 :, :] = jnp.zeros((2, depth - offsets // 8 * 8, wide * LANES), jnp.float32)
    lanes = pl.ds(pl.multiple_of(zi * wide * LANES, LANES), wide * LANES)
    for part in range(2):
        source = tables_any.at[:, part, lanes]
        load = pltpu.make_async_copy(source, table.at[part, pl.ds(0, offsets)], sems.at[part])
        load.start()
        loads.append(load)
    chosen = []
    for s in range(zc):
        first = pl.multiple_of(((zi ^ s) * rest + ci) * par_cnt, par_cnt)
        words = words_ref[pl.ds(first, par_cnt), :]
        which, offset = words & 0xFFFF, lax.shift_right_logical(words, 16)
        rows = []
        for slot in range(slots):
            here = slice(slot * par_cnt, (slot + 1) * par_cnt)
            pick_ref[s, here, :] = one_hot(which[:, slot : slot + 1], total_cnt)
            rows.append(one_hot(offset[:, slot : slot + 1], depth))
        chosen.append(jnp.concatenate(rows, 0))
    for load in loads:
        load.wait()
    for w in range(wide):
        here = slice(w * LANES, (w + 1) * LANES)
        both = jnp.concatenate([table[0, :, here], table[1, :, here]], 1).astype(jnp.bfloat16)
        for s in range(zc):
            factor = jnp.dot(chosen[s], both, preferred_element_type=jnp.float32)
            factor_ref[w, s, 0] = factor[:, :LANES]
            factor_ref[w, s, 1] = factor[:, LANES:]


def prepare(zc, rest, wide, words, tables):
    total_cnt, slots = words.shape
    rows = slots * total_cnt // (zc * rest)
    depth = -(-tables.shape[0] // LANES) * LANES
    return pl.pallas_call(
        functools.partial(prepare_kernel, zc, rest, wide),
        out_shape=[
            jax.ShapeDtypeStruct((zc, rows, total_cnt), jnp.bfloat16),
            jax.ShapeDtypeStruct((wide, zc, 2, rows, LANES), jnp.float32),
        ],
        in_specs=[VMEM, FAR],
        out_specs=[VMEM, VMEM],
        scratch_shapes=[
            pltpu.VMEM((2, depth, wide * LANES), jnp.float32),
            pltpu.SemaphoreType.DMA((2,)),
        ],
        compiler_params=GRANT,
        name="prepare",
    )(words, tables)


def swap_rows(outer, inner):
    rows = outer * inner
    row = lax.broadcasted_iota(jnp.int32, (rows, rows), 0)
    source = lax.broadcasted_iota(jnp.int32, (rows, rows), 1)
    wanted = row % outer * inner + row // outer
    return jnp.where(source == wanted, 1.0, 0.0).astype(jnp.bfloat16)


def add_partners(targets, w, par_cnt, pick_ref, factor_ref, source, outs):
    cols = source.shape[0]
    half = cols // 2
    slots = pick_ref.shape[1] // par_cnt
    swap = swap_rows(cols, par_cnt)
    for s, out_ref in zip(targets, outs):
        left, right = [], []
        for col in range(half):
            pair = jnp.concatenate([source[col], source[col + half]], 1)
            found = jnp.dot(pick_ref[s], pair, preferred_element_type=jnp.float32)
            for slot in range(slots):
                here = slice(slot * par_cnt, (slot + 1) * par_cnt)
                a, b = found[here, :LANES], found[here, LANES:]
                c, d = factor_ref[w, s, 0, here, :], factor_ref[w, s, 1, here, :]
                re, im = a * c - b * d, a * d + b * c
                real = re if slot == 0 else real + re
                imag = im if slot == 0 else imag + im
            left.append(real)
            right.append(imag)
        total = jnp.concatenate(left + right, 0).astype(jnp.bfloat16)
        moved = jnp.dot(swap, total, preferred_element_type=jnp.float32)
        out_ref[...] = moved.astype(jnp.bfloat16).reshape(out_ref.shape)


def first_translate_kernel(zc, rest, targets, w, pick_ref, factor_ref, *refs):
    pieces = refs[: -1 - len(targets)]
    outs, source = refs[-1 - len(targets) : -1], refs[-1]
    par_cnt, cols = outs[0].shape[:2]
    each = len(pieces) // zc
    _, zi, ci = places(rest)
    swap = swap_rows(par_cnt, cols)
    for s in range(zc):
        for t in range(each):
            box = (zi ^ s) * rest + ((ci ^ t) if each > 1 else 0)
            piece = pieces[s * each + t]

            def place(k, carry, box=box, piece=piece):
                rows = piece[pl.ds(k * par_cnt, par_cnt)].reshape(par_cnt * cols, LANES)
                moved = jnp.dot(swap, rows, preferred_element_type=jnp.float32)
                moved = moved.astype(jnp.bfloat16).reshape(cols, par_cnt, LANES)
                first = pl.multiple_of((box + k) * par_cnt, par_cnt)
                source[:, pl.ds(first, par_cnt), :] = moved
                return carry

            count = piece.shape[0] // par_cnt
            if count == 1:
                place(0, 0)
            else:
                lax.fori_loop(0, count, place, 0)
    add_partners(targets, w, par_cnt, pick_ref, factor_ref, source, outs)


def translate_kernel(targets, w, pick_ref, factor_ref, source, *outs):
    par_cnt = outs[0].shape[0]
    add_partners(targets, w, par_cnt, pick_ref, factor_ref, source, outs)


def translate(zc, rest, w, par_cnt, groups, picks, factors, pieces):
    cols, lanes = pieces[0].shape[1:]
    out = jax.ShapeDtypeStruct((par_cnt, cols, lanes), jnp.bfloat16)
    found = {}
    source = None
    for targets in groups:
        if source is None:
            result = pl.pallas_call(
                functools.partial(first_translate_kernel, zc, rest, targets, w),
                out_shape=[out] * len(targets)
                + [jax.ShapeDtypeStruct((cols, zc * rest * par_cnt, lanes), jnp.bfloat16)],
                in_specs=[VMEM, VMEM] + [VMEM] * len(pieces),
                out_specs=[VMEM] * (len(targets) + 1),
                compiler_params=GRANT,
                name="first_translate",
            )(picks, factors, *pieces)
            source = result[-1]
        else:
            call = pl.pallas_call(
                functools.partial(translate_kernel, targets, w),
                out_shape=[out] * len(targets),
                in_specs=[VMEM, VMEM, VMEM],
                out_specs=[VMEM] * len(targets),
                compiler_params=GRANT,
                name="translate",
            )
            result = call(picks, factors, source)
        for s, value in zip(targets, result):
            found[s] = value
    return [found[s] for s in range(zc)]


def backward_kernel(mask, wide, rest, last, interp_ref, cos_ref, sin_ref, quarter, *refs):
    held, out_ref = (refs[0] if len(refs) == 2 else None), refs[-1]
    chunks, par_cnt, cols, _ = quarter.shape
    width = chunks * LANES
    span, block = min(chunks, 2), min(par_cnt, 4)
    sign = half_sign(cols, 1.0)
    dir_at, zi, _ = places(rest)
    lane_sets = []
    for chunk in range(chunks):
        place = (zi ^ (chunk // wide)) * wide + chunk % wide
        start = (dir_at ^ mask) * width + place * LANES
        lane_sets.append(pl.ds(pl.multiple_of(start, LANES), LANES))
    for first in range(0, par_cnt, block):
        here = slice(first * CH * cols, (first + block) * CH * cols)
        total = None if held is None else held[here, :]
        for base in range(0, chunks, span):
            left, right = [], []
            for chunk in range(base, base + span):
                lanes = lane_sets[chunk]
                rows = []
                for p in range(first, first + block):
                    field = quarter[chunk, p].astype(jnp.float32)
                    turned = sign * pltpu.roll(field, cols // 2, 0)
                    for o in range(CH):
                        rows.append(field * cos_ref[o : o + 1, lanes] + turned * sin_ref[o : o + 1, lanes])
                left.append(jnp.concatenate(rows, 0).astype(jnp.bfloat16))
                right.append(interp_ref[:, lanes])
            part = lax.dot_general(
                jnp.concatenate(left, 1),
                jnp.concatenate(right, 1),
                (((1,), (1,)), ((), ())),
                preferred_element_type=jnp.float32,
            )
            total = part if total is None else total + part
        if last:
            total = anterp_scale * total
        out_ref[here, :] = total.astype(out_ref.dtype)


def backward(mask, wide, rest, last, interp, cosine, sine, quarter, held):
    _, par_cnt, cols, _ = quarter.shape
    rows = par_cnt * CH * cols
    kept = [] if held is None else [held]
    return pl.pallas_call(
        functools.partial(backward_kernel, mask, wide, rest, last),
        out_shape=jax.ShapeDtypeStruct(
            (rows, interp.shape[0]), jnp.bfloat16 if last else jnp.float32
        ),
        in_specs=[VMEM, VMEM, VMEM, VMEM] + [VMEM] * len(kept),
        out_specs=VMEM,
        compiler_params=GRANT,
        name="backward",
    )(interp, cosine, sine, quarter, *kept)


def far(value):
    return pltpu.with_memory_space_constraint(value, pltpu.HBM)


def exchange(value, axis, mask):
    size = lax.axis_size(axis)
    return lax.ppermute(value, axis, [(i, i ^ mask) for i in range(size)])


def per_device(child_out, interp, shift_angle, translators, nbr_index, nbr_trans):
    child_cnt, cols, kq = child_out.shape
    par_cnt = child_cnt // CH
    npd = interp.shape[1]
    ndir, nbox = lax.axis_size("dir"), lax.axis_size("box")
    jq = npd // ndir
    zc = 1
    while nbox % (2 * zc) == 0 and zc * 2 < nbox and jq % (2 * zc * LANES) == 0:
        zc *= 2
    rest = nbox // zc
    chunks = jq // LANES
    wide = chunks // zc
    zi = lax.axis_index("box") // rest
    x = child_out.reshape(child_cnt * cols, kq)
    masks = tuple(range(ndir - 1, 0, -1))

    part, x, mine, cosine, sine = first_forward(
        masks[0], chunks, cols, far(x), far(interp), far(shift_angle)
    )
    arrived = [exchange(part, "dir", masks[0])]
    for mask in masks[1:]:
        part = forward(mask, chunks, cols, x, mine, cosine, sine)
        arrived.append(exchange(part, "dir", mask))
    total = forward(0, chunks, cols, x, mine, cosine, sine)
    words = nbr_index | (nbr_trans << 16)
    picks, factors = prepare(zc, rest, wide, words, far(translators))
    for part in arrived:
        total = total + part.astype(jnp.float32)
    own = total.astype(jnp.bfloat16).reshape(zc, wide, par_cnt, cols, LANES)

    pieces = []
    for s in range(zc):
        piece = lax.dynamic_index_in_dim(own, zi ^ s, 0, keepdims=False)
        pieces.append(exchange(piece, "box", s * rest) if s else piece)
    if rest == 2:
        pieces = [part for piece in pieces for part in (piece, exchange(piece, "box", 1))]
    else:
        groups = [[z * rest + c for c in range(rest)] for z in range(zc)]
        pieces = [
            lax.all_gather(piece, "box", axis=1, tiled=True, axis_index_groups=groups)
            for piece in pieces
        ]

    order = [(s,) for s in range(zc - 1, -1, -1)]
    back = []
    for w in range(wide):
        parts = [piece[w] for piece in pieces]
        back.append(translate(zc, rest, w, par_cnt, order, picks, factors, parts))
    quarter = []
    for s in range(zc):
        result = jnp.stack([b[s] for b in back])
        quarter.append(exchange(result, "box", s * rest) if s else result)
    quarter = jnp.concatenate(quarter, 0)

    received = [exchange(quarter, "dir", mask) for mask in range(1, ndir)]
    out = backward(0, wide, rest, ndir == 1, mine, cosine, sine, quarter, None)
    for mask, quarter in zip(range(1, ndir), received):
        out = backward(mask, wide, rest, mask == ndir - 1, mine, cosine, sine, quarter, out)
    return out.reshape(child_cnt, cols, kq)


def solution(mesh):
    in_specs = (P("box", None, "dir"), P(), P(), P(None, None, "dir"), P(), P())
    out_specs = P("box", None, "dir")

    return jax.shard_map(
        per_device, mesh=mesh, in_specs=in_specs, out_specs=out_specs, check_vma=False
    )
```

```python
import functools

import jax
import jax.numpy as jnp
from jax import lax
from jax.experimental import pallas as pl
from jax.experimental.pallas import tpu as pltpu
from jax.sharding import PartitionSpec as P


CH = 8
LANES = 128
anterp_scale = 0.125
HALF_PI = 1.5707963267948966
HALF_PI_HIGH = 1.57080078125
HALF_PI_LOW = HALF_PI - HALF_PI_HIGH

VMEM = pl.BlockSpec(memory_space=pltpu.VMEM)
SMEM = pl.BlockSpec(memory_space=pltpu.SMEM)
FAR = pl.BlockSpec(memory_space=pltpu.HBM)
GRANT = pltpu.CompilerParams(vmem_limit_bytes=12 << 20)


def places(rest):
    box_at = lax.axis_index("box")
    return lax.axis_index("dir"), box_at // rest, box_at % rest


def half_sign(rows, first):
    row = lax.broadcasted_iota(jnp.int32, (rows, LANES), 0)
    return jnp.where(row < rows // 2, first, -first).astype(jnp.float32)


def sine_cosine(angle):
    turns = jnp.round(angle * (1.0 / HALF_PI))
    x = (angle - turns * HALF_PI_HIGH) - turns * HALF_PI_LOW
    y = x * x
    s = x * (1.0 + y * (-1.6666654611e-1 + y * (8.3321608736e-3 + y * -1.9515295891e-4)))
    c = 1.0 + y * (
        -0.5 + y * (4.166664568298827e-2 + y * (-1.388731625493765e-3 + y * 2.443315711809948e-5))
    )
    quadrant = turns.astype(jnp.int32)
    odd = (quadrant & 1) == 1
    sine = jnp.where(odd, c, s)
    cosine = jnp.where(odd, s, c)
    sine = jnp.where((quadrant & 2) == 2, -sine, sine)
    cosine = jnp.where(((quadrant + 1) & 2) == 2, -cosine, cosine)
    return sine, cosine


def add_octants(x_ref, interp_ref, angle_ref, start, out_ref, cos_ref, sin_ref):
    chunks, par_cnt, cols, _ = out_ref.shape
    width = chunks * LANES
    span = min(chunks, 2)
    sign = half_sign(cols, -1.0)
    sine_all, cosine_all = sine_cosine(angle_ref[:, pl.ds(start, width)])
    cos_ref[...] = cosine_all
    sin_ref[...] = sine_all
    for base in range(0, chunks, span):
        at = pl.multiple_of(start + base * LANES, LANES)
        field = jnp.dot(
            x_ref[...], interp_ref[:, pl.ds(at, span * LANES)], preferred_element_type=jnp.float32
        )
        for chunk in range(span):
            here = slice((base + chunk) * LANES, (base + chunk + 1) * LANES)
            cosine = [jnp.broadcast_to(cos_ref[o : o + 1, here], (cols, LANES)) for o in range(CH)]
            sine = [jnp.broadcast_to(sin_ref[o : o + 1, here], (cols, LANES)) for o in range(CH)]
            for p in range(par_cnt):
                same = cross = None
                for o in range(CH):
                    row = (p * CH + o) * cols
                    part = field[row : row + cols, chunk * LANES : (chunk + 1) * LANES]
                    same = part * cosine[o] if o == 0 else same + part * cosine[o]
                    cross = part * sine[o] if o == 0 else cross + part * sine[o]
                total = same + sign * pltpu.roll(cross, cols // 2, 0)
                out_ref[base + chunk, p] = total.astype(out_ref.dtype)


def first_kernel(mask, x_any, interp_any, angle_any, *refs):
    out_ref, cos_ref, sin_ref, x_ref, interp_ref, angle_ref, sems = refs
    width = out_ref.shape[0] * LANES
    rows = interp_ref.shape[0]
    dir_at = lax.axis_index("dir")
    start = pl.multiple_of((dir_at ^ mask) * width, width)
    mine = pl.ds(pl.multiple_of(dir_at * rows, rows), rows)
    loads = [
        pltpu.make_async_copy(angle_any, angle_ref, sems.at[0]),
        pltpu.make_async_copy(x_any, x_ref, sems.at[1]),
    ]
    for step in range(interp_ref.shape[1] // width):
        at = pl.multiple_of((dir_at ^ mask ^ step) * width, width)
        here = interp_ref.at[:, pl.ds(at, width)]
        loads.append(
            pltpu.make_async_copy(interp_any.at[mine, pl.ds(at, width)], here, sems.at[2 + step])
        )
    for load in loads:
        load.start()
    for load in loads[:3]:
        load.wait()
    add_octants(x_ref, interp_ref, angle_ref, start, out_ref, cos_ref, sin_ref)
    for load in loads[3:]:
        load.wait()


def quarter_shapes(chunks, par_cnt, cols, kind):
    table = jax.ShapeDtypeStruct((CH, chunks * LANES), jnp.float32)
    return [jax.ShapeDtypeStruct((chunks, par_cnt, cols, LANES), kind), table, table]


def first_forward(mask, chunks, cols, x, interp, angle):
    rows, kq = x.shape
    npd = interp.shape[1]
    par_cnt = rows // (CH * cols)
    return pl.pallas_call(
        functools.partial(first_kernel, mask),
        out_shape=quarter_shapes(chunks, par_cnt, cols, jnp.bfloat16)
        + [
            jax.ShapeDtypeStruct(x.shape, x.dtype),
            jax.ShapeDtypeStruct((kq, npd), interp.dtype),
            jax.ShapeDtypeStruct(angle.shape, jnp.float32),
        ],
        in_specs=[FAR, FAR, FAR],
        out_specs=[VMEM] * 6,
        scratch_shapes=[pltpu.SemaphoreType.DMA((2 + npd // (chunks * LANES),))],
        compiler_params=GRANT,
        name="first_forward",
    )(x, interp, angle)


def forward_kernel(mask, x_ref, interp_ref, angle_ref, out_ref, cos_ref, sin_ref):
    width = out_ref.shape[0] * LANES
    start = pl.multiple_of((lax.axis_index("dir") ^ mask) * width, width)
    add_octants(x_ref, interp_ref, angle_ref, start, out_ref, cos_ref, sin_ref)


def forward(mask, chunks, cols, x, interp, angle):
    par_cnt = x.shape[0] // (CH * cols)
    kind = jnp.bfloat16 if mask else jnp.float32
    return pl.pallas_call(
        functools.partial(forward_kernel, mask),
        out_shape=quarter_shapes(chunks, par_cnt, cols, kind),
        in_specs=[VMEM, VMEM, VMEM],
        out_specs=[VMEM] * 3,
        compiler_params=GRANT,
        name="forward",
    )(x, interp, angle)


def one_hot(column, count):
    lane = lax.broadcasted_iota(jnp.int32, (column.shape[0], count), 1)
    return jnp.where(lane == column, 1.0, 0.0).astype(jnp.bfloat16)


def prepare_kernel(zc, rest, wide, words_ref, tables_any, *refs):
    pick_ref, factor_ref, table, sems = refs
    total_cnt, slots = words_ref.shape
    par_cnt = total_cnt // (zc * rest)
    offsets, depth = tables_any.shape[0], table.shape[1]
    _, zi, ci = places(rest)
    loads = []
    table[:, offsets // 8 * 8 :, :] = jnp.zeros((2, depth - offsets // 8 * 8, wide * LANES), jnp.float32)
    lanes = pl.ds(pl.multiple_of(zi * wide * LANES, LANES), wide * LANES)
    for part in range(2):
        source = tables_any.at[:, part, lanes]
        load = pltpu.make_async_copy(source, table.at[part, pl.ds(0, offsets)], sems.at[part])
        load.start()
        loads.append(load)
    chosen = []
    for s in range(zc):
        first = pl.multiple_of(((zi ^ s) * rest + ci) * par_cnt, par_cnt)
        words = words_ref[pl.ds(first, par_cnt), :]
        which, offset = words & 0xFFFF, lax.shift_right_logical(words, 16)
        rows = []
        for slot in range(slots):
            here = slice(slot * par_cnt, (slot + 1) * par_cnt)
            pick_ref[s, here, :] = one_hot(which[:, slot : slot + 1], total_cnt)
            rows.append(one_hot(offset[:, slot : slot + 1], depth))
        chosen.append(jnp.concatenate(rows, 0))
    for load in loads:
        load.wait()
    for w in range(wide):
        here = slice(w * LANES, (w + 1) * LANES)
        both = jnp.concatenate([table[0, :, here], table[1, :, here]], 1).astype(jnp.bfloat16)
        for s in range(zc):
            factor = jnp.dot(chosen[s], both, preferred_element_type=jnp.float32)
            factor_ref[w, s, 0] = factor[:, :LANES]
            factor_ref[w, s, 1] = factor[:, LANES:]


def prepare(zc, rest, wide, words, tables):
    total_cnt, slots = words.shape
    rows = slots * total_cnt // (zc * rest)
    depth = -(-tables.shape[0] // LANES) * LANES
    return pl.pallas_call(
        functools.partial(prepare_kernel, zc, rest, wide),
        out_shape=[
            jax.ShapeDtypeStruct((zc, rows, total_cnt), jnp.bfloat16),
            jax.ShapeDtypeStruct((wide, zc, 2, rows, LANES), jnp.float32),
        ],
        in_specs=[VMEM, FAR],
        out_specs=[VMEM, VMEM],
        scratch_shapes=[
            pltpu.VMEM((2, depth, wide * LANES), jnp.float32),
            pltpu.SemaphoreType.DMA((2,)),
        ],
        compiler_params=GRANT,
        name="prepare",
    )(words, tables)


def swap_rows(outer, inner):
    rows = outer * inner
    row = lax.broadcasted_iota(jnp.int32, (rows, rows), 0)
    source = lax.broadcasted_iota(jnp.int32, (rows, rows), 1)
    wanted = row % outer * inner + row // outer
    return jnp.where(source == wanted, 1.0, 0.0).astype(jnp.bfloat16)


def add_partners(targets, w, par_cnt, pick_ref, factor_ref, source, outs):
    cols = source.shape[0]
    half = cols // 2
    slots = pick_ref.shape[1] // par_cnt
    swap = swap_rows(cols, par_cnt)
    for s, out_ref in zip(targets, outs):
        left, right = [], []
        for col in range(half):
            pair = jnp.concatenate([source[col], source[col + half]], 1)
            found = jnp.dot(pick_ref[s], pair, preferred_element_type=jnp.float32)
            for slot in range(slots):
                here = slice(slot * par_cnt, (slot + 1) * par_cnt)
                a, b = found[here, :LANES], found[here, LANES:]
                c, d = factor_ref[w, s, 0, here, :], factor_ref[w, s, 1, here, :]
                re, im = a * c - b * d, a * d + b * c
                real = re if slot == 0 else real + re
                imag = im if slot == 0 else imag + im
            left.append(real)
            right.append(imag)
        total = jnp.concatenate(left + right, 0).astype(jnp.bfloat16)
        moved = jnp.dot(swap, total, preferred_element_type=jnp.float32)
        out_ref[...] = moved.astype(jnp.bfloat16).reshape(out_ref.shape)


def first_translate_kernel(zc, rest, targets, w, pick_ref, factor_ref, *refs):
    pieces = refs[: -1 - len(targets)]
    outs, source = refs[-1 - len(targets) : -1], refs[-1]
    par_cnt, cols = outs[0].shape[:2]
    each = len(pieces) // zc
    _, zi, ci = places(rest)
    swap = swap_rows(par_cnt, cols)
    for s in range(zc):
        for t in range(each):
            box = (zi ^ s) * rest + ((ci ^ t) if each > 1 else 0)
            piece = pieces[s * each + t]

            def place(k, carry, box=box, piece=piece):
                rows = piece[pl.ds(k * par_cnt, par_cnt)].reshape(par_cnt * cols, LANES)
                moved = jnp.dot(swap, rows, preferred_element_type=jnp.float32)
                moved = moved.astype(jnp.bfloat16).reshape(cols, par_cnt, LANES)
                first = pl.multiple_of((box + k) * par_cnt, par_cnt)
                source[:, pl.ds(first, par_cnt), :] = moved
                return carry

            count = piece.shape[0] // par_cnt
            if count == 1:
                place(0, 0)
            else:
                lax.fori_loop(0, count, place, 0)
    add_partners(targets, w, par_cnt, pick_ref, factor_ref, source, outs)


def translate_kernel(targets, w, pick_ref, factor_ref, source, *outs):
    par_cnt = outs[0].shape[0]
    add_partners(targets, w, par_cnt, pick_ref, factor_ref, source, outs)


def translate(zc, rest, w, par_cnt, groups, picks, factors, pieces):
    cols, lanes = pieces[0].shape[1:]
    out = jax.ShapeDtypeStruct((par_cnt, cols, lanes), jnp.bfloat16)
    found = {}
    source = None
    for targets in groups:
        if source is None:
            result = pl.pallas_call(
                functools.partial(first_translate_kernel, zc, rest, targets, w),
                out_shape=[out] * len(targets)
                + [jax.ShapeDtypeStruct((cols, zc * rest * par_cnt, lanes), jnp.bfloat16)],
                in_specs=[VMEM, VMEM] + [VMEM] * len(pieces),
                out_specs=[VMEM] * (len(targets) + 1),
                compiler_params=GRANT,
                name="first_translate",
            )(picks, factors, *pieces)
            source = result[-1]
        else:
            call = pl.pallas_call(
                functools.partial(translate_kernel, targets, w),
                out_shape=[out] * len(targets),
                in_specs=[VMEM, VMEM, VMEM],
                out_specs=[VMEM] * len(targets),
                compiler_params=GRANT,
                name="translate",
            )
            result = call(picks, factors, source)
        for s, value in zip(targets, result):
            found[s] = value
    return [found[s] for s in range(zc)]


def backward_kernel(mask, wide, rest, last, interp_ref, cos_ref, sin_ref, quarter, *refs):
    refs = list(refs)
    sems = refs.pop() if last else None
    kept = refs.pop() if last else None
    out_ref = refs.pop()
    held = refs.pop() if refs else None
    chunks, par_cnt, cols, _ = quarter.shape
    width = chunks * LANES
    span, block = min(chunks, 2), min(par_cnt, 4)
    sign = half_sign(cols, 1.0)
    dir_at, zi, _ = places(rest)
    near, far_sets = [], []
    for chunk in range(chunks):
        place = ((zi ^ (chunk // wide)) * wide + chunk % wide) * LANES
        near.append(pl.ds(pl.multiple_of(place, LANES), LANES))
        far_sets.append(pl.ds(pl.multiple_of((dir_at ^ mask) * width + place, LANES), LANES))
    stores = []
    for first in range(0, par_cnt, block):
        here = slice(first * CH * cols, (first + block) * CH * cols)
        total = None if held is None else held[here, :]
        for base in range(0, chunks, span):
            left, right = [], []
            for chunk in range(base, base + span):
                lanes = near[chunk]
                rows = []
                for p in range(first, first + block):
                    field = quarter[chunk, p].astype(jnp.float32)
                    turned = sign * pltpu.roll(field, cols // 2, 0)
                    for o in range(CH):
                        rows.append(field * cos_ref[o : o + 1, lanes] + turned * sin_ref[o : o + 1, lanes])
                left.append(jnp.concatenate(rows, 0).astype(jnp.bfloat16))
                right.append(interp_ref[:, far_sets[chunk]])
            part = lax.dot_general(
                jnp.concatenate(left, 1),
                jnp.concatenate(right, 1),
                (((1,), (1,)), ((), ())),
                preferred_element_type=jnp.float32,
            )
            total = part if total is None else total + part
        if last:
            kept[here, :] = (anterp_scale * total).astype(kept.dtype)
            store = pltpu.make_async_copy(
                kept.at[here, :], out_ref.at[here, :], sems.at[first // block]
            )
            store.start()
            stores.append(store)
        else:
            out_ref[here, :] = total
    for store in stores:
        store.wait()


def backward(mask, wide, rest, last, interp, tables, quarter, held):
    _, par_cnt, cols, _ = quarter.shape
    shape = (par_cnt * CH * cols, interp.shape[0])
    kept = [] if held is None else [held]
    if last:
        out_shape = jax.ShapeDtypeStruct(shape, jnp.bfloat16)
        scratch = [pltpu.VMEM(shape, jnp.bfloat16), pltpu.SemaphoreType.DMA((-(-par_cnt // 4),))]
    else:
        out_shape, scratch = jax.ShapeDtypeStruct(shape, jnp.float32), []
    return pl.pallas_call(
        functools.partial(backward_kernel, mask, wide, rest, last),
        out_shape=out_shape,
        in_specs=[VMEM, VMEM, VMEM, VMEM] + [VMEM] * len(kept),
        out_specs=FAR if last else VMEM,
        scratch_shapes=scratch,
        compiler_params=GRANT,
        name="backward",
    )(interp, *tables, quarter, *kept)


def far(value):
    return pltpu.with_memory_space_constraint(value, pltpu.HBM)


def exchange(value, axis, mask):
    size = lax.axis_size(axis)
    return lax.ppermute(value, axis, [(i, i ^ mask) for i in range(size)])


def per_device(child_out, interp, shift_angle, translators, nbr_index, nbr_trans):
    child_cnt, cols, kq = child_out.shape
    par_cnt = child_cnt // CH
    npd = interp.shape[1]
    ndir, nbox = lax.axis_size("dir"), lax.axis_size("box")
    chunks, zc, rest = splits(npd, ndir, nbox)
    wide = chunks // zc
    zi = lax.axis_index("box") // rest
    x = child_out.reshape(child_cnt * cols, kq)
    masks = tuple(range(ndir - 1, 0, -1))

    part, *turns, x, mine, angle = first_forward(
        masks[0], chunks, cols, far(x), far(interp), far(shift_angle)
    )
    tables = {masks[0]: turns}
    arrived = [exchange(part, "dir", masks[0])]
    for mask in masks[1:]:
        part, *tables[mask] = forward(mask, chunks, cols, x, mine, angle)
        arrived.append(exchange(part, "dir", mask))
    total, *tables[0] = forward(0, chunks, cols, x, mine, angle)
    words = nbr_index | (nbr_trans << 16)
    picks, factors = prepare(zc, rest, wide, words, far(translators))
    for part in arrived:
        total = total + part.astype(jnp.float32)
    own = total.astype(jnp.bfloat16).reshape(zc, wide, par_cnt, cols, LANES)

    pieces = []
    for s in range(zc):
        piece = lax.dynamic_index_in_dim(own, zi ^ s, 0, keepdims=False)
        pieces.append(exchange(piece, "box", s * rest) if s else piece)
    if rest == 2:
        pieces = [part for piece in pieces for part in (piece, exchange(piece, "box", 1))]
    else:
        groups = [[z * rest + c for c in range(rest)] for z in range(zc)]
        pieces = [
            lax.all_gather(piece, "box", axis=1, tiled=True, axis_index_groups=groups)
            for piece in pieces
        ]

    order = [(s,) for s in home_order(zc)]
    back = []
    for w in range(wide):
        parts = [piece[w] for piece in pieces]
        back.append(translate(zc, rest, w, par_cnt, order, picks, factors, parts))
    quarter = []
    for s in range(zc):
        result = jnp.stack([b[s] for b in back])
        quarter.append(exchange(result, "box", s * rest) if s else result)
    quarter = jnp.concatenate(quarter, 0)

    received = [exchange(quarter, "dir", mask) for mask in range(1, ndir)]
    out = backward(0, wide, rest, ndir == 1, mine, tables[0], quarter, None)
    for mask, quarter in zip(range(1, ndir), received):
        out = backward(mask, wide, rest, mask == ndir - 1, mine, tables[mask], quarter, out)
    return out.reshape(child_cnt, cols, kq)


def splits(npd, ndir, nbox):
    jq, zc = npd // ndir, 1
    while nbox % (2 * zc) == 0 and zc * 2 < nbox and jq % (2 * zc * LANES) == 0:
        zc *= 2
    return jq // LANES, zc, nbox // zc


def home_order(zc):
    return ((zc - 1,) + tuple(range(1, zc - 1)) if zc > 1 else ()) + (0,)


def solution(mesh):
    in_specs = (P("box", None, "dir"), P(), P(), P(None, None, "dir"), P(), P())
    out_specs = P("box", None, "dir")

    def run(*args):
        ndir, nbox = mesh.shape["dir"], mesh.shape["box"]
        _, _, _ = splits(args[1].shape[1], ndir, nbox)
        step = jax.shard_map(
            per_device, mesh=mesh, in_specs=in_specs, out_specs=out_specs, check_vma=False
        )
        return step(*args)

    return run
```

```python
import functools

import jax
import jax.numpy as jnp
from jax import lax
from jax.experimental import pallas as pl
from jax.experimental.pallas import tpu as pltpu
from jax.sharding import PartitionSpec as P


CH = 8
LANES = 128
anterp_scale = 0.125
HALF_PI = 1.5707963267948966
HALF_PI_HIGH = 1.57080078125
HALF_PI_LOW = HALF_PI - HALF_PI_HIGH

VMEM = pl.BlockSpec(memory_space=pltpu.VMEM)
SMEM = pl.BlockSpec(memory_space=pltpu.SMEM)
FAR = pl.BlockSpec(memory_space=pltpu.HBM)
GRANT = pltpu.CompilerParams(vmem_limit_bytes=12 << 20)


def side(rest, s):
    return 1 if s and rest == 2 else 0


def places(rest):
    box_at = lax.axis_index("box")
    return lax.axis_index("dir"), box_at // rest, box_at % rest


def half_sign(rows, first):
    row = lax.broadcasted_iota(jnp.int32, (rows, LANES), 0)
    return jnp.where(row < rows // 2, first, -first).astype(jnp.float32)


def sine_cosine(angle):
    turns = jnp.round(angle * (1.0 / HALF_PI))
    x = (angle - turns * HALF_PI_HIGH) - turns * HALF_PI_LOW
    y = x * x
    s = x * (1.0 + y * (-1.6666654611e-1 + y * (8.3321608736e-3 + y * -1.9515295891e-4)))
    c = 1.0 + y * (
        -0.5 + y * (4.166664568298827e-2 + y * (-1.388731625493765e-3 + y * 2.443315711809948e-5))
    )
    quadrant = turns.astype(jnp.int32)
    odd = (quadrant & 1) == 1
    sine = jnp.where(odd, c, s)
    cosine = jnp.where(odd, s, c)
    sine = jnp.where((quadrant & 2) == 2, -sine, sine)
    cosine = jnp.where(((quadrant + 1) & 2) == 2, -cosine, cosine)
    return sine, cosine


def add_octants(x_ref, interp_ref, angle_ref, start, out_ref, cos_ref, sin_ref):
    chunks, par_cnt, cols, _ = out_ref.shape
    width = chunks * LANES
    span = min(chunks, 2)
    sign = half_sign(cols, -1.0)
    sine_all, cosine_all = sine_cosine(angle_ref[:, pl.ds(start, width)])
    cos_ref[...] = cosine_all
    sin_ref[...] = sine_all
    for base in range(0, chunks, span):
        at = pl.multiple_of(start + base * LANES, LANES)
        field = jnp.dot(
            x_ref[...], interp_ref[:, pl.ds(at, span * LANES)], preferred_element_type=jnp.float32
        )
        for chunk in range(span):
            here = slice((base + chunk) * LANES, (base + chunk + 1) * LANES)
            cosine = [jnp.broadcast_to(cos_ref[o : o + 1, here], (cols, LANES)) for o in range(CH)]
            sine = [jnp.broadcast_to(sin_ref[o : o + 1, here], (cols, LANES)) for o in range(CH)]
            for p in range(par_cnt):
                same = cross = None
                for o in range(CH):
                    row = (p * CH + o) * cols
                    part = field[row : row + cols, chunk * LANES : (chunk + 1) * LANES]
                    same = part * cosine[o] if o == 0 else same + part * cosine[o]
                    cross = part * sine[o] if o == 0 else cross + part * sine[o]
                total = same + sign * pltpu.roll(cross, cols // 2, 0)
                out_ref[base + chunk, p] = total.astype(out_ref.dtype)


def first_kernel(mask, x_any, interp_any, angle_any, *refs):
    out_ref, cos_ref, sin_ref, x_ref, interp_ref, angle_ref, sems = refs
    width = out_ref.shape[0] * LANES
    rows = interp_ref.shape[0]
    dir_at = lax.axis_index("dir")
    start = pl.multiple_of((dir_at ^ mask) * width, width)
    mine = pl.ds(pl.multiple_of(dir_at * rows, rows), rows)
    loads = [
        pltpu.make_async_copy(angle_any, angle_ref, sems.at[0]),
        pltpu.make_async_copy(x_any, x_ref, sems.at[1]),
    ]
    for step in range(interp_ref.shape[1] // width):
        at = pl.multiple_of((dir_at ^ mask ^ step) * width, width)
        here = interp_ref.at[:, pl.ds(at, width)]
        loads.append(
            pltpu.make_async_copy(interp_any.at[mine, pl.ds(at, width)], here, sems.at[2 + step])
        )
    for load in loads:
        load.start()
    for load in loads[:3]:
        load.wait()
    add_octants(x_ref, interp_ref, angle_ref, start, out_ref, cos_ref, sin_ref)
    for load in loads[3:]:
        load.wait()


def quarter_shapes(chunks, par_cnt, cols, kind):
    table = jax.ShapeDtypeStruct((CH, chunks * LANES), jnp.float32)
    return [jax.ShapeDtypeStruct((chunks, par_cnt, cols, LANES), kind), table, table]


def first_forward(mask, chunks, cols, x, interp, angle):
    rows, kq = x.shape
    npd = interp.shape[1]
    par_cnt = rows // (CH * cols)
    return pl.pallas_call(
        functools.partial(first_kernel, mask),
        out_shape=quarter_shapes(chunks, par_cnt, cols, jnp.bfloat16)
        + [
            jax.ShapeDtypeStruct(x.shape, x.dtype),
            jax.ShapeDtypeStruct((kq, npd), interp.dtype),
            jax.ShapeDtypeStruct(angle.shape, jnp.float32),
        ],
        in_specs=[FAR, FAR, FAR],
        out_specs=[VMEM] * 6,
        scratch_shapes=[pltpu.SemaphoreType.DMA((2 + npd // (chunks * LANES),))],
        compiler_params=GRANT,
        name="first_forward",
    )(x, interp, angle)


def forward_kernel(mask, x_ref, interp_ref, angle_ref, out_ref, cos_ref, sin_ref):
    width = out_ref.shape[0] * LANES
    start = pl.multiple_of((lax.axis_index("dir") ^ mask) * width, width)
    add_octants(x_ref, interp_ref, angle_ref, start, out_ref, cos_ref, sin_ref)


def forward(mask, chunks, cols, x, interp, angle):
    par_cnt = x.shape[0] // (CH * cols)
    kind = jnp.bfloat16 if mask else jnp.float32
    return pl.pallas_call(
        functools.partial(forward_kernel, mask),
        out_shape=quarter_shapes(chunks, par_cnt, cols, kind),
        in_specs=[VMEM, VMEM, VMEM],
        out_specs=[VMEM] * 3,
        compiler_params=GRANT,
        name="forward",
    )(x, interp, angle)


def one_hot(column, count):
    lane = lax.broadcasted_iota(jnp.int32, (column.shape[0], count), 1)
    return jnp.where(lane == column, 1.0, 0.0).astype(jnp.bfloat16)


def prepare_kernel(zc, rest, wide, words_ref, tables_any, *refs):
    pick_ref, factor_ref, table, sems = refs
    total_cnt, slots = words_ref.shape
    par_cnt = total_cnt // (zc * rest)
    offsets, depth = tables_any.shape[0], table.shape[1]
    _, zi, ci = places(rest)
    loads = []
    table[:, offsets // 8 * 8 :, :] = jnp.zeros((2, depth - offsets // 8 * 8, wide * LANES), jnp.float32)
    lanes = pl.ds(pl.multiple_of(zi * wide * LANES, LANES), wide * LANES)
    for part in range(2):
        source = tables_any.at[:, part, lanes]
        load = pltpu.make_async_copy(source, table.at[part, pl.ds(0, offsets)], sems.at[part])
        load.start()
        loads.append(load)
    chosen = []
    for s in range(zc):
        first = ((zi ^ s) * rest + ci) * par_cnt
        first = pl.multiple_of(first, par_cnt)
        words = words_ref[pl.ds(first, par_cnt), :]
        which, offset = words & 0xFFFF, lax.shift_right_logical(words, 16)
        rows = []
        for slot in range(slots):
            here = slice(slot * par_cnt, (slot + 1) * par_cnt)
            pick_ref[s, here, :] = one_hot(which[:, slot : slot + 1], total_cnt)
            rows.append(one_hot(offset[:, slot : slot + 1], depth))
        chosen.append(jnp.concatenate(rows, 0))
    for load in loads:
        load.wait()
    for w in range(wide):
        here = slice(w * LANES, (w + 1) * LANES)
        both = jnp.concatenate([table[0, :, here], table[1, :, here]], 1).astype(jnp.bfloat16)
        for s in range(zc):
            factor = jnp.dot(chosen[s], both, preferred_element_type=jnp.float32)
            factor_ref[w, s, 0] = factor[:, :LANES]
            factor_ref[w, s, 1] = factor[:, LANES:]


def prepare(zc, rest, wide, words, tables):
    total_cnt, slots = words.shape
    rows = slots * total_cnt // (zc * rest)
    depth = -(-tables.shape[0] // LANES) * LANES
    return pl.pallas_call(
        functools.partial(prepare_kernel, zc, rest, wide),
        out_shape=[
            jax.ShapeDtypeStruct((zc, rows, total_cnt), jnp.bfloat16),
            jax.ShapeDtypeStruct((wide, zc, 2, rows, LANES), jnp.float32),
        ],
        in_specs=[VMEM, FAR],
        out_specs=[VMEM, VMEM],
        scratch_shapes=[
            pltpu.VMEM((2, depth, wide * LANES), jnp.float32),
            pltpu.SemaphoreType.DMA((2,)),
        ],
        compiler_params=GRANT,
        name="prepare",
    )(words, tables)


def swap_rows(outer, inner):
    rows = outer * inner
    row = lax.broadcasted_iota(jnp.int32, (rows, rows), 0)
    source = lax.broadcasted_iota(jnp.int32, (rows, rows), 1)
    wanted = row % outer * inner + row // outer
    return jnp.where(source == wanted, 1.0, 0.0).astype(jnp.bfloat16)


def add_partners(targets, w, par_cnt, pick_ref, factor_ref, source, outs):
    cols = source.shape[0]
    half = cols // 2
    slots = pick_ref.shape[1] // par_cnt
    swap = swap_rows(cols, par_cnt)
    for s, out_ref in zip(targets, outs):
        left, right = [], []
        for col in range(half):
            pair = jnp.concatenate([source[col], source[col + half]], 1)
            found = jnp.dot(pick_ref[s], pair, preferred_element_type=jnp.float32)
            for slot in range(slots):
                here = slice(slot * par_cnt, (slot + 1) * par_cnt)
                a, b = found[here, :LANES], found[here, LANES:]
                c, d = factor_ref[w, s, 0, here, :], factor_ref[w, s, 1, here, :]
                re, im = a * c - b * d, a * d + b * c
                real = re if slot == 0 else real + re
                imag = im if slot == 0 else imag + im
            left.append(real)
            right.append(imag)
        total = jnp.concatenate(left + right, 0).astype(jnp.bfloat16)
        moved = jnp.dot(swap, total, preferred_element_type=jnp.float32)
        out_ref[...] = moved.astype(jnp.bfloat16).reshape(out_ref.shape)


def first_translate_kernel(zc, rest, targets, w, pick_ref, factor_ref, *refs):
    pieces = refs[: -1 - len(targets)]
    outs, source = refs[-1 - len(targets) : -1], refs[-1]
    par_cnt, cols = outs[0].shape[:2]
    each = len(pieces) // zc
    _, zi, ci = places(rest)
    swap = swap_rows(par_cnt, cols)
    for s in range(zc):
        for t in range(each):
            box = (zi ^ s) * rest + ((ci ^ t ^ side(rest, s)) if each > 1 else 0)
            piece = pieces[s * each + t]

            def place(k, carry, box=box, piece=piece):
                rows = piece[pl.ds(k * par_cnt, par_cnt)].reshape(par_cnt * cols, LANES)
                moved = jnp.dot(swap, rows, preferred_element_type=jnp.float32)
                moved = moved.astype(jnp.bfloat16).reshape(cols, par_cnt, LANES)
                first = pl.multiple_of((box + k) * par_cnt, par_cnt)
                source[:, pl.ds(first, par_cnt), :] = moved
                return carry

            count = piece.shape[0] // par_cnt
            if count == 1:
                place(0, 0)
            else:
                lax.fori_loop(0, count, place, 0)
    add_partners(targets, w, par_cnt, pick_ref, factor_ref, source, outs)


def translate_kernel(targets, w, pick_ref, factor_ref, source, *outs):
    par_cnt = outs[0].shape[0]
    add_partners(targets, w, par_cnt, pick_ref, factor_ref, source, outs)


def translate(zc, rest, w, par_cnt, groups, picks, factors, pieces):
    cols, lanes = pieces[0].shape[1:]
    out = jax.ShapeDtypeStruct((par_cnt, cols, lanes), jnp.bfloat16)
    found = {}
    source = None
    for targets in groups:
        if source is None:
            result = pl.pallas_call(
                functools.partial(first_translate_kernel, zc, rest, targets, w),
                out_shape=[out] * len(targets)
                + [jax.ShapeDtypeStruct((cols, zc * rest * par_cnt, lanes), jnp.bfloat16)],
                in_specs=[VMEM, VMEM] + [VMEM] * len(pieces),
                out_specs=[VMEM] * (len(targets) + 1),
                compiler_params=GRANT,
                name="first_translate",
            )(picks, factors, *pieces)
            source = result[-1]
        else:
            call = pl.pallas_call(
                functools.partial(translate_kernel, targets, w),
                out_shape=[out] * len(targets),
                in_specs=[VMEM, VMEM, VMEM],
                out_specs=[VMEM] * len(targets),
                compiler_params=GRANT,
                name="translate",
            )
            result = call(picks, factors, source)
        for s, value in zip(targets, result):
            found[s] = value
    return [found[s] for s in range(zc)]


def backward_kernel(mask, wide, rest, last, interp_ref, cos_ref, sin_ref, quarter, *refs):
    refs = list(refs)
    sems = refs.pop() if last else None
    kept = refs.pop() if last else None
    out_ref = refs.pop()
    held = refs.pop() if refs else None
    chunks, par_cnt, cols, _ = quarter.shape
    width = chunks * LANES
    span, block = min(chunks, 2), min(par_cnt, 4)
    sign = half_sign(cols, 1.0)
    dir_at, zi, _ = places(rest)
    near, far_sets = [], []
    for chunk in range(chunks):
        place = ((zi ^ (chunk // wide)) * wide + chunk % wide) * LANES
        near.append(pl.ds(pl.multiple_of(place, LANES), LANES))
        far_sets.append(pl.ds(pl.multiple_of((dir_at ^ mask) * width + place, LANES), LANES))
    stores = []
    for first in range(0, par_cnt, block):
        here = slice(first * CH * cols, (first + block) * CH * cols)
        total = None if held is None else held[here, :]
        for base in range(0, chunks, span):
            left, right = [], []
            for chunk in range(base, base + span):
                lanes = near[chunk]
                rows = []
                for p in range(first, first + block):
                    field = quarter[chunk, p].astype(jnp.float32)
                    turned = sign * pltpu.roll(field, cols // 2, 0)
                    for o in range(CH):
                        rows.append(field * cos_ref[o : o + 1, lanes] + turned * sin_ref[o : o + 1, lanes])
                left.append(jnp.concatenate(rows, 0).astype(jnp.bfloat16))
                right.append(interp_ref[:, far_sets[chunk]])
            part = lax.dot_general(
                jnp.concatenate(left, 1),
                jnp.concatenate(right, 1),
                (((1,), (1,)), ((), ())),
                preferred_element_type=jnp.float32,
            )
            total = part if total is None else total + part
        if last:
            kept[here, :] = (anterp_scale * total).astype(kept.dtype)
            store = pltpu.make_async_copy(
                kept.at[here, :], out_ref.at[here, :], sems.at[first // block]
            )
            store.start()
            stores.append(store)
        else:
            out_ref[here, :] = total
    for store in stores:
        store.wait()


def backward(mask, wide, rest, last, interp, tables, quarter, held):
    _, par_cnt, cols, _ = quarter.shape
    shape = (par_cnt * CH * cols, interp.shape[0])
    kept = [] if held is None else [held]
    if last:
        out_shape = jax.ShapeDtypeStruct(shape, jnp.bfloat16)
        scratch = [pltpu.VMEM(shape, jnp.bfloat16), pltpu.SemaphoreType.DMA((-(-par_cnt // 4),))]
    else:
        out_shape, scratch = jax.ShapeDtypeStruct(shape, jnp.float32), []
    return pl.pallas_call(
        functools.partial(backward_kernel, mask, wide, rest, last),
        out_shape=out_shape,
        in_specs=[VMEM, VMEM, VMEM, VMEM] + [VMEM] * len(kept),
        out_specs=FAR if last else VMEM,
        scratch_shapes=scratch,
        compiler_params=GRANT,
        name="backward",
    )(interp, *tables, quarter, *kept)


def far(value):
    return pltpu.with_memory_space_constraint(value, pltpu.HBM)


def exchange(value, axis, mask):
    size = lax.axis_size(axis)
    return lax.ppermute(value, axis, [(i, i ^ mask) for i in range(size)])


def per_device(child_out, interp, shift_angle, translators, nbr_index, nbr_trans):
    child_cnt, cols, kq = child_out.shape
    par_cnt = child_cnt // CH
    npd = interp.shape[1]
    ndir, nbox = lax.axis_size("dir"), lax.axis_size("box")
    chunks, zc, rest = splits(npd, ndir, nbox)
    wide = chunks // zc
    zi = lax.axis_index("box") // rest
    x = child_out.reshape(child_cnt * cols, kq)
    masks = down_order(ndir)

    part, *turns, x, mine, angle = first_forward(
        masks[0], chunks, cols, far(x), far(interp), far(shift_angle)
    )
    tables = {masks[0]: turns}
    arrived = [exchange(part, "dir", masks[0])]
    for mask in masks[1:]:
        part, *tables[mask] = forward(mask, chunks, cols, x, mine, angle)
        arrived.append(exchange(part, "dir", mask))
    total, *tables[0] = forward(0, chunks, cols, x, mine, angle)
    words = nbr_index | (nbr_trans << 16)
    picks, factors = prepare(zc, rest, wide, words, far(translators))
    for part in arrived:
        total = total + part.astype(jnp.float32)
    own = total.astype(jnp.bfloat16).reshape(zc, wide, par_cnt, cols, LANES)

    pieces = []
    for s in range(zc):
        piece = lax.dynamic_index_in_dim(own, zi ^ s, 0, keepdims=False)
        pieces.append(exchange(piece, "box", s * rest + side(rest, s)) if s else piece)
    if rest == 2:
        pieces = [part for piece in pieces for part in (piece, exchange(piece, "box", 1))]
    else:
        groups = [[z * rest + c for c in range(rest)] for z in range(zc)]
        pieces = [
            lax.all_gather(piece, "box", axis=1, tiled=True, axis_index_groups=groups)
            for piece in pieces
        ]

    order = [(s,) for s in home_order(zc)]
    back = []
    for w in range(wide):
        parts = [piece[w] for piece in pieces]
        back.append(translate(zc, rest, w, par_cnt, order, picks, factors, parts))
    quarter = []
    for s in range(zc):
        result = jnp.stack([b[s] for b in back])
        quarter.append(exchange(result, "box", s * rest) if s else result)
    quarter = jnp.concatenate(quarter, 0)

    down = down_order(ndir)
    received = [exchange(quarter, "dir", mask) for mask in down]
    out = backward(0, wide, rest, ndir == 1, mine, tables[0], quarter, None)
    for mask, quarter in zip(down, received):
        out = backward(mask, wide, rest, mask == down[-1], mine, tables[mask], quarter, out)
    return out.reshape(child_cnt, cols, kq)


def splits(npd, ndir, nbox):
    jq, zc = npd // ndir, 1
    while nbox % (2 * zc) == 0 and zc * 2 < nbox and jq % (2 * zc * LANES) == 0:
        zc *= 2
    return jq // LANES, zc, nbox // zc


def home_order(zc):
    return tuple(range(zc - 1, 0, -1)) + (0,)


def down_order(ndir):
    return (ndir - 1,) + tuple(range(1, ndir - 1))


def solution(mesh):
    in_specs = (P("box", None, "dir"), P(), P(), P(None, None, "dir"), P(), P())
    out_specs = P("box", None, "dir")

    def run(*args):
        ndir, nbox = mesh.shape["dir"], mesh.shape["box"]
        _, _, _ = splits(args[1].shape[1], ndir, nbox)
        step = jax.shard_map(
            per_device, mesh=mesh, in_specs=in_specs, out_specs=out_specs, check_vma=False
        )
        return step(*args)

    return run
```
